32 devices in a mesh: groups: 2 (over y), row: 8 (over z, x), col: 2 (over core).
Axes of the slice: x: 2, y: 2, z: 4, core: 2. Of those that a mesh axis runs over, the one named last changes fastest.
Arguments:
- gram_old: bfloat16 [28672, 14336], P(('groups', 'row'), 'col'), parts along dimension 0, may hold values from -10 to 256, as said below
- activations: bfloat16 [256, 14336], P('groups', 'row'), parts along dimension 0, may hold values from -0.5 to 0.5
- weights: float32 [14336, 512], P('row', ('groups', 'col')), parts along dimension 1, may hold values from -6 to 6
- block_mask: int32 [112, 4], P(None, 'groups'), parts along dimension 1, may hold values 0 or 1
Outputs:
- pruned: float32 [14336, 512], P('row', ('groups', 'col')), parts along dimension 1
The draws below stay inside these ranges and needn't reach their ends.
There are 2 independent parts, one for each index of `groups`. The reference program is written for one: setup_inputs(seed, part) draws one part's arguments, and reference() takes and returns one part's arrays. A program takes and returns all parts, laid end to end along the dimension named above; each array names one. Nothing has to cross between parts.
Inputs may be any that keep to these rules, and one draw needn't show every extreme that they name: `gram_old`: symmetric and positive definite.
All inputs are finite; a program needn't handle non-finite values.
Results may differ from the reference program's by a relative error of at most 0.00076.
Values may be sent and summed in bfloat16 or wider, within the bound.
A program may use at most 128 MiB of HBM per device.

```python
import math
import jax
import jax.numpy as jnp

K = 14336
BLK = 128
NCOL = 256
ROWS = 128
KB = 112
NB = 2


def draw_gram_old(key, part):
    key_noise = jax.random.fold_in(key, 11)
    key_scale = jax.random.fold_in(key, 23)
    noise = jax.random.normal(key_noise, (K, K), jnp.float32)
    symmetric = (noise + noise.T) * (1.0 / math.sqrt(2.0 * K))
    base = 3.0 * jnp.eye(K, dtype=jnp.float32) + symmetric
    position = jnp.arange(K, dtype=jnp.float32) / K
    uniform_draw = jax.random.uniform(key_scale, (K,), jnp.float32)
    squares = jnp.exp(uniform_draw * math.log(10.0)) * (1.0 + 2.0 * position)
    scales = jnp.sqrt(squares)
    return (scales[:, None] * base * scales[None, :]).astype(jnp.bfloat16)


def place_ends(values, stream_key, least, largest):
    shape = values.shape
    spot = [jax.random.randint(jax.random.fold_in(stream_key, axis), (), 0, shape[axis]) for axis in range(len(shape))]
    values = values.at[tuple(spot)].set(least)
    longest = shape.index(max(shape))
    spot[longest] = (spot[longest] + 1) % shape[longest]
    return values.at[tuple(spot)].set(largest)


def block_scale(stream_key, dims, split, smallest, largest):
    level, own = 1.0, jax.random.fold_in(stream_key, 6)
    for dim, parts in split:
        steps = jnp.exp(jax.random.uniform(jax.random.fold_in(own, dim), (parts,), jnp.float32, smallest / len(split), largest / len(split)))
        level = level * jnp.repeat(steps, dims[dim] // parts).reshape([-1 if axis == dim else 1 for axis in range(len(dims))])
    return level


def bell_draw(key, dims, deviation, limit, cuts=(), kind=jnp.bfloat16):
    factor_of = block_scale(key, dims, cuts, -0.22, 0.18) if cuts else 1.0
    result = jax.random.normal(key, dims, jnp.float32) * deviation * factor_of
    return jnp.minimum(jnp.maximum(result, -limit), limit).astype(kind)


def setup_inputs(seed: int = 0, part: int = 0) -> dict:
    splits = jax.random.split(jax.random.key(seed), 5)
    part_keys = jax.random.split(jax.random.fold_in(splits[4], part), 5)
    gram_old = draw_gram_old(jax.random.fold_in(jax.random.fold_in(splits[4], part), 71), part)
    activations = bell_draw(part_keys[1], (ROWS, K), ROWS ** -0.5, 0.5, ((1, 8),))
    weights = bell_draw(part_keys[2], (K, NCOL), 1.0, 6.0, ((0, 8), (1, 2)), jnp.float32)
    block_mask = place_ends((jax.random.randint(part_keys[3], (KB, NB), 0, 2) < 1).astype(jnp.int32), jax.random.fold_in(part_keys[3], 1), 0, 1)
    return {"gram_old": gram_old, "activations": activations, "weights": weights, "block_mask": block_mask}


damping_ratio = 0.3
epsilon = 1e-6


def expand_mask(block_mask):
    widened = jnp.repeat(block_mask.astype(jnp.float32), BLK, axis=0)
    return jnp.repeat(widened, BLK, axis=1)


def reference(gram_old, activations, weights, block_mask):
    gram_update = jnp.dot(activations.T, activations, preferred_element_type=jnp.float32)
    gram_new = (gram_old.astype(jnp.float32) + gram_update).astype(jnp.bfloat16)
    trace_total = jnp.sum(jnp.diagonal(gram_new).astype(jnp.float32))
    damping = damping_ratio * trace_total / K
    mask_full = expand_mask(block_mask)
    kept_weights = mask_full * weights
    pruned_diff = kept_weights - weights
    grad_first = jnp.dot(gram_new, pruned_diff.astype(jnp.bfloat16), preferred_element_type=jnp.float32)
    step_dir = mask_full * grad_first
    curvature = jnp.dot(gram_new, step_dir.astype(jnp.bfloat16), preferred_element_type=jnp.float32)
    masked_curve = mask_full * curvature
    grad_square = jnp.sum(step_dir * step_dir)
    grad_curve = jnp.sum(step_dir * curvature)
    curve_square = jnp.sum(masked_curve * masked_curve)
    step_first = grad_square / (grad_curve + damping * grad_square + epsilon)
    step_second = (grad_curve + damping * grad_square) / (curve_square + 2.0 * damping * grad_curve + damping * damping * grad_square + epsilon)
    grad_second = grad_first - step_first * curvature
    return kept_weights - step_first * step_dir - step_second * (mask_full * grad_second)
```

```python
import jax
import jax.numpy as jnp
from jax import lax
from jax.sharding import PartitionSpec as P

K = 14336
BLK = 128


damping_ratio = 0.3
epsilon = 1e-06


def partner(value, axis, distance):
    return lax.ppermute(value, axis, [(i, i ^ 1 << distance) for i in range(lax.axis_size(axis))])


def expand_local(block_mask, row_offset, row_count, col_offset, col_count):
    row_ids = (row_offset + jnp.arange(row_count, dtype=jnp.int32)) // BLK
    col_ids = (col_offset + jnp.arange(col_count, dtype=jnp.int32)) // BLK
    pick_rows = (
        row_ids[:, None] == jnp.arange(block_mask.shape[0], dtype=jnp.int32)[None, :]
    ).astype(jnp.float32)
    pick_cols = (
        col_ids[:, None] == jnp.arange(block_mask.shape[1], dtype=jnp.int32)[None, :]
    ).astype(jnp.float32)
    partial_rows = jnp.dot(
        pick_rows, block_mask.astype(jnp.float32), precision=lax.Precision.HIGHEST
    )
    return jnp.dot(partial_rows, pick_cols.T, precision=lax.Precision.HIGHEST)


def update_product(activations, inner):
    high = inner.astype(jnp.bfloat16)
    low = (inner - high.astype(jnp.float32)).astype(jnp.bfloat16)
    contract = (((0,), (0,)), ((), ()))
    return lax.dot_general(
        activations, high, contract, preferred_element_type=jnp.float32
    ) + lax.dot_general(activations, low, contract, preferred_element_type=jnp.float32)


def per_device(gram_old, activations, weights, block_mask):
    row_block = gram_old.shape[0]
    half_width = gram_old.shape[1]
    width_cols = weights.shape[1]
    row_index = lax.axis_index("row")
    col_index = lax.axis_index("col")
    row_offset = row_index * row_block
    half_offset = col_index * half_width
    diag_column = row_offset + jnp.arange(row_block, dtype=jnp.int32) - half_offset
    on_diagonal = jnp.arange(half_width, dtype=jnp.int32)[None, :] == diag_column[:, None]
    trace_part = jnp.sum(jnp.where(on_diagonal, gram_old.astype(jnp.float32), 0.0))
    acts_wide = activations.astype(jnp.float32)
    trace_part = trace_part + jnp.sum(acts_wide * acts_wide) / lax.axis_size("col")
    mask_local = expand_local(block_mask, row_offset, row_block, col_index * width_cols, width_cols)

    def apply_gram(panel):
        panel_low = panel.astype(jnp.bfloat16)
        inner = lax.psum(
            jnp.dot(activations, panel_low, preferred_element_type=jnp.float32), "row"
        )
        low_rank = update_product(activations, inner)
        column_panel = lax.all_gather(panel_low, "row", axis=0, tiled=True)
        own_half = lax.dynamic_slice_in_dim(column_panel, half_offset, half_width, 0)
        partner_need = lax.dynamic_slice_in_dim(
            column_panel, (1 - col_index) * half_width, half_width, 0
        )
        partner_half = partner(partner_need, "col", 0)
        own_part = jnp.dot(gram_old, own_half, preferred_element_type=jnp.float32)
        partner_part = jnp.dot(gram_old, partner_half, preferred_element_type=jnp.float32)
        return own_part + partner(partner_part, "col", 0) + low_rank

    kept_weights = mask_local * weights
    pruned_diff = kept_weights - weights
    grad_first = apply_gram(pruned_diff)
    step_dir = mask_local * grad_first
    curvature = apply_gram(step_dir)
    masked_curve = mask_local * curvature
    local_square = jnp.sum(step_dir * step_dir)
    local_curve = jnp.sum(step_dir * curvature)
    local_curve_square = jnp.sum(masked_curve * masked_curve)
    grad_square, grad_curve, curve_square, trace_total = lax.psum(
        jnp.stack([local_square, local_curve, local_curve_square, trace_part]), ("row", "col")
    )
    damping = damping_ratio * trace_total / K
    step_first = grad_square / (grad_curve + damping * grad_square + epsilon)
    step_second = (grad_curve + damping * grad_square) / (
        curve_square + 2.0 * damping * grad_curve + damping * damping * grad_square + epsilon
    )
    grad_second = grad_first - step_first * curvature
    return kept_weights - step_first * step_dir - step_second * (mask_local * grad_second)


def solution(mesh):
    placed = (
        P(("groups", "row"), "col"),
        P("groups", "row"),
        P("row", ("groups", "col")),
        P(None, "groups"),
    )
    return jax.shard_map(
        per_device,
        mesh=mesh,
        in_specs=placed,
        out_specs=P("row", ("groups", "col")),
        check_vma=False,
    )
```

```python
import functools

import jax
import jax.numpy as jnp
from jax import lax
from jax.experimental import pallas as pl
from jax.experimental.pallas import tpu as pltpu
from jax.sharding import PartitionSpec as P

BLK = 128
CHUNK = 2 * BLK
MESH = pl.DeviceIdType.MESH
TRANSPOSED = (((0,), (0,)), ((), ()))


damping_ratio = 0.3
epsilon = 1e-06


def partner(value, axis, distance):
    return lax.ppermute(value, axis, [(i, i ^ 1 << distance) for i in range(lax.axis_size(axis))])


def expand_local(block_mask, row_offset, row_count, col_offset, col_count):
    row_ids = (row_offset + jnp.arange(row_count, dtype=jnp.int32)) // BLK
    col_ids = (col_offset + jnp.arange(col_count, dtype=jnp.int32)) // BLK
    pick_rows = (
        row_ids[:, None] == jnp.arange(block_mask.shape[0], dtype=jnp.int32)[None, :]
    ).astype(jnp.float32)
    pick_cols = (
        col_ids[:, None] == jnp.arange(block_mask.shape[1], dtype=jnp.int32)[None, :]
    ).astype(jnp.float32)
    partial_rows = jnp.dot(
        pick_rows, block_mask.astype(jnp.float32), precision=lax.Precision.HIGHEST
    )
    return jnp.dot(partial_rows, pick_cols.T, precision=lax.Precision.HIGHEST)


def update_product(activations, inner):
    high = inner.astype(jnp.bfloat16)
    low = (inner - high.astype(jnp.float32)).astype(jnp.bfloat16)
    contract = (((0,), (0,)), ((), ()))
    return lax.dot_general(
        activations, high, contract, preferred_element_type=jnp.float32
    ) + lax.dot_general(activations, low, contract, preferred_element_type=jnp.float32)


def per_device(gram_old, activations, weights, block_mask):
    row_block = gram_old.shape[0]
    half_width = gram_old.shape[1]
    width_cols = weights.shape[1]
    row_index = lax.axis_index("row")
    col_index = lax.axis_index("col")
    row_offset = row_index * row_block
    half_offset = col_index * half_width
    diag_column = row_offset + jnp.arange(row_block, dtype=jnp.int32) - half_offset
    on_diagonal = jnp.arange(half_width, dtype=jnp.int32)[None, :] == diag_column[:, None]
    trace_part = jnp.sum(jnp.where(on_diagonal, gram_old.astype(jnp.float32), 0.0))
    acts_wide = activations.astype(jnp.float32)
    trace_part = trace_part + jnp.sum(acts_wide * acts_wide) / lax.axis_size("col")
    mask_local = expand_local(block_mask, row_offset, row_block, col_index * width_cols, width_cols)

    def apply_gram(panel):
        panel_low = panel.astype(jnp.bfloat16)
        inner = lax.psum(
            jnp.dot(activations, panel_low, preferred_element_type=jnp.float32), "row"
        )
        low_rank = update_product(activations, inner)
        column_panel = lax.all_gather(panel_low, "row", axis=0, tiled=True)
        own_half = lax.dynamic_slice_in_dim(column_panel, half_offset, half_width, 0)
        partner_need = lax.dynamic_slice_in_dim(
            column_panel, (1 - col_index) * half_width, half_width, 0
        )
        partner_half = partner(partner_need, "col", 0)
        own_part = jnp.dot(gram_old, own_half, preferred_element_type=jnp.float32)
        partner_part = jnp.dot(gram_old, partner_half, preferred_element_type=jnp.float32)
        return own_part + partner(partner_part, "col", 0) + low_rank

    kept_weights = mask_local * weights
    pruned_diff = kept_weights - weights
    grad_first = apply_gram(pruned_diff)
    step_dir = mask_local * grad_first
    curvature = apply_gram(step_dir)
    masked_curve = mask_local * curvature
    local_square = jnp.sum(step_dir * step_dir)
    local_curve = jnp.sum(step_dir * curvature)
    local_curve_square = jnp.sum(masked_curve * masked_curve)
    grad_square, grad_curve, curve_square, trace_total = lax.psum(
        jnp.stack([local_square, local_curve, local_curve_square, trace_part]), ("row", "col")
    )
    damping = damping_ratio * trace_total / (row_block * lax.axis_size("row"))
    step_first = grad_square / (grad_curve + damping * grad_square + epsilon)
    step_second = (grad_curve + damping * grad_square) / (
        curve_square + 2.0 * damping * grad_curve + damping * damping * grad_square + epsilon
    )
    grad_second = grad_first - step_first * curvature
    return kept_weights - step_first * step_dir - step_second * (mask_local * grad_second)


def fused_kernel(
    n, gram, acts, weights, mask, out,
    g_vm, xo, xp, y_own, y_oth, y_rx, grad, rs_send, rs_recv, ag_send, ag_recv,
    trace_row, tot_send, tot_recv,
    g_sem, ring_ssem, ring_rsem, par_ssem, par_rsem, y_ssem, y_rsem,
    rs_ssem, rs_rsem, ag_ssem, ag_rsem, tot_ssem, tot_rsem,
):
    rows, width = weights.shape
    nb = gram.shape[1] // rows
    nz = n // 2
    chunks = rows // CHUNK
    split = (chunks + 1) // 2
    last = n // 2 - 1
    piece = rs_send.shape[2]
    blocks = rows // BLK
    group = lax.axis_index("groups")
    row = lax.axis_index("row")
    col = lax.axis_index("col")
    near_half = row // nb

    def row_of(place):
        place = lax.rem(place + 2 * n, n)
        x = place // nz
        z = place + x * (n - 1 - 2 * place)
        return 2 * z + x

    my_z, my_x = row // 2, lax.rem(row, 2)
    place = my_z + my_x * (n - 1 - 2 * my_z)
    right, left = row_of(place + 1), row_of(place - 1)

    def mask_at(block):
        return mask[row * blocks + block, col].astype(jnp.float32)

    def ring(phase, way, hop, j):
        source = row_of(place - hop) if way == 0 else row_of(place + hop)
        part = xo.at[phase, source, pl.ds(pl.multiple_of(j * CHUNK, CHUNK), CHUNK)]
        return pltpu.make_async_remote_copy(
            src_ref=part, dst_ref=part,
            send_sem=ring_ssem.at[phase, way, hop, j], recv_sem=ring_rsem.at[phase, way, hop, j],
            device_id=(group, right if way == 0 else left, col), device_id_type=MESH,
        )

    def ring_arrival(phase, way, hop, j):
        source = row_of(place - hop - 1) if way == 0 else row_of(place + hop + 1)
        part = xo.at[phase, source, pl.ds(pl.multiple_of(j * CHUNK, CHUNK), CHUNK)]
        return pltpu.make_async_remote_copy(
            src_ref=part, dst_ref=part,
            send_sem=ring_ssem.at[phase, way, hop, j], recv_sem=ring_rsem.at[phase, way, hop, j],
            device_id=(group, right if way == 0 else left, col), device_id_type=MESH,
        )

    def to_partner(phase, source, j):
        span = pl.ds(pl.multiple_of(j * CHUNK, CHUNK), CHUNK)
        return pltpu.make_async_remote_copy(
            src_ref=xo.at[phase, source, span], dst_ref=xp.at[phase, lax.rem(source, nb), span],
            send_sem=par_ssem.at[phase, lax.rem(source, nb), j],
            recv_sem=par_rsem.at[phase, lax.rem(source, nb), j],
            device_id=(group, row, 1 - col), device_id_type=MESH,
        )

    def y_copy(phase, j):
        span = pl.ds(pl.multiple_of(j * CHUNK, CHUNK), CHUNK)
        return pltpu.make_async_remote_copy(
            src_ref=y_oth.at[phase, span], dst_ref=y_rx.at[phase, span],
            send_sem=y_ssem.at[phase, j], recv_sem=y_rsem.at[phase, j],
            device_id=(group, row, 1 - col), device_id_type=MESH,
        )

    def rs_copy(phase, peer, slot):
        return pltpu.make_async_remote_copy(
            src_ref=rs_send.at[phase, peer], dst_ref=rs_recv.at[phase, slot],
            send_sem=rs_ssem.at[phase, peer], recv_sem=rs_rsem.at[phase, slot],
            device_id=(group, peer, col), device_id_type=MESH,
        )

    def ag_copy(phase, peer, slot):
        return pltpu.make_async_remote_copy(
            src_ref=ag_send.at[phase], dst_ref=ag_recv.at[phase, slot],
            send_sem=ag_ssem.at[phase, peer], recv_sem=ag_rsem.at[phase, slot],
            device_id=(group, peer, col), device_id_type=MESH,
        )

    me = row * 2 + col

    def tot_copy(peer, slot):
        return pltpu.make_async_remote_copy(
            src_ref=tot_send, dst_ref=tot_recv.at[slot],
            send_sem=tot_ssem.at[peer], recv_sem=tot_rsem.at[slot],
            device_id=(group, peer // 2, lax.rem(peer, 2)), device_id_type=MESH,
        )

    def send_own(phase, j):
        @pl.when(near_half != col)
        def _():
            to_partner(phase, row, j).start()

        ring(phase, 0, 0, j).start()
        ring(phase, 1, 0, j).start()

    def send_inner(phase):
        inner = jnp.dot(
            acts[...], xo[phase, row], preferred_element_type=jnp.float32
        )
        for peer in range(n):
            rs_send[phase, peer] = inner[peer * piece:(peer + 1) * piece]
        for k in range(1, n):
            rs_copy(phase, lax.rem(row + k, n), row).start()

    def share_inner(phase):
        total = rs_send[phase, row]
        for k in range(1, n):
            peer = lax.rem(row + k, n)
            rs_copy(phase, peer, peer).wait_recv()
            total = total + rs_recv[phase, peer]
        ag_send[phase] = total
        ag_recv[phase, row] = total
        for k in range(1, n):
            ag_copy(phase, lax.rem(row + k, n), row).start()

    def get_inner(phase):
        for k in range(1, n):
            peer = lax.rem(row + k, n)
            ag_copy(phase, peer, peer).wait_recv()
        inner = ag_recv[phase].reshape(n * piece, width)
        high = inner.astype(jnp.bfloat16)
        low = (inner - high.astype(jnp.float32)).astype(jnp.bfloat16)
        return jnp.concatenate([high, low], axis=1)

    def process(phase, source, j):
        @pl.when(source // nb != col)
        def _():
            @pl.when(source != row)
            def _():
                to_partner(phase, source, j).start()

        @pl.when(source // nb == col)
        def _():
            to_partner(phase, source, j).wait_recv()
            span = pl.ds(pl.multiple_of(j * CHUNK, CHUNK), CHUNK)
            block = lax.rem(source, nb)
            panel = jnp.concatenate([xo[phase, source, span], xp[phase, block, span]], axis=1)

            @pl.loop(0, 2)
            def _(tile):
                at = pl.ds(pl.multiple_of(tile * (rows // 2), rows // 2), rows // 2)
                got = jnp.dot(
                    g_vm[block, at, span], panel, preferred_element_type=jnp.float32
                )
                y_own[at] += got[:, :width]
                y_oth[phase, at] += got[:, width:]

    def gather_and_multiply(phase):
        for hop in range(last):
            if hop == min(1, last - 1):
                share_inner(phase)

            @pl.loop(0, chunks)
            def _(j):
                for way in range(2):
                    ring_arrival(phase, way, hop, j).wait_recv()
                    if hop + 1 < last:
                        ring(phase, way, hop + 1, j).start()
                    else:
                        @pl.when(j < split if way == 0 else j >= split)
                        def _():
                            ring(phase, way, hop + 1, j).start()
                process(phase, row_of(place - hop - 1), j)
                process(phase, row_of(place + hop + 1), j)
                if hop == min(1, last - 1):
                    process(phase, row, j)

        far = row_of(place + n // 2)

        @pl.loop(0, chunks)
        def _(j):
            @pl.when(j < split)
            def _():
                ring_arrival(phase, 0, last, j).wait_recv()

            @pl.when(j >= split)
            def _():
                ring_arrival(phase, 1, last, j).wait_recv()

            @pl.when(far // nb != col)
            def _():
                to_partner(phase, far, j).start()

        block = lax.rem(far, nb)

        @pl.when(far // nb == col)
        def _():
            @pl.loop(0, chunks)
            def _(j):
                to_partner(phase, far, j).wait_recv()

            panel = jnp.concatenate([xo[phase, far], xp[phase, block]], axis=1)

            @pl.loop(0, chunks)
            def _(j):
                at = pl.ds(pl.multiple_of(j * CHUNK, CHUNK), CHUNK)
                got = jnp.dot(g_vm[block, at], panel, preferred_element_type=jnp.float32)
                y_own[at] += got[:, :width]
                y_oth[phase, at] += got[:, width:]
                y_copy(phase, j).start()

        @pl.when(far // nb != col)
        def _():
            @pl.loop(0, chunks)
            def _(j):
                y_copy(phase, j).start()

    def product(phase, j, inner):
        y_copy(phase, j).wait_recv()
        span = pl.ds(pl.multiple_of(j * CHUNK, CHUNK), CHUNK)
        both = lax.dot_general(
            acts[:, span], inner, TRANSPOSED, preferred_element_type=jnp.float32
        )
        return y_own[span] + y_rx[phase, span] + (both[:, :width] + both[:, width:])

    def fold(values):
        return jnp.sum(values.reshape(-1, 8, width), axis=0)

    for b in range(nb):
        pltpu.make_async_copy(
            gram.at[:, pl.ds(b * rows, rows)], g_vm.at[b], g_sem.at[b]
        ).start()
    barrier = pltpu.get_barrier_semaphore()
    for k in range(1, 2 * n):
        peer = lax.rem(me + k, 2 * n)
        pl.semaphore_signal(
            barrier, inc=1, device_id=(group, peer // 2, lax.rem(peer, 2)), device_id_type=MESH
        )
    for i in range(blocks):
        at = pl.ds(i * BLK, BLK)
        w = weights[at]
        xo[0, row, at] = (mask_at(i) * w - w).astype(jnp.bfloat16)
    y_own[...] = jnp.zeros_like(y_own)
    y_oth[...] = jnp.zeros_like(y_oth)
    pl.semaphore_wait(barrier, 2 * n - 1)
    send_inner(0)

    @pl.loop(0, chunks)
    def _(j):
        send_own(0, j)

    for b in range(nb):
        pltpu.make_async_copy(
            gram.at[:, pl.ds(b * rows, rows)], g_vm.at[b], g_sem.at[b]
        ).wait()

    trace_row[...] = jnp.zeros_like(trace_row)

    @pl.when(near_half == col)
    def _():
        own = lax.rem(row, nb)
        eye = lax.broadcasted_iota(jnp.int32, (BLK, BLK), 0) == lax.broadcasted_iota(
            jnp.int32, (BLK, BLK), 1
        )
        total = jnp.zeros((1, BLK), jnp.float32)
        for i in range(blocks):
            at = pl.ds(i * BLK, BLK)
            diagonal = jnp.where(eye, g_vm[own, at, at].astype(jnp.float32), 0.0)
            act = acts[:, at].astype(jnp.float32)
            total = total + jnp.sum(diagonal, axis=0, keepdims=True) + jnp.sum(
                act * act, axis=0, keepdims=True
            )
        trace_row[0:1] = total

    gather_and_multiply(0)
    inner = get_inner(0)

    @pl.loop(0, chunks)
    def _(j):
        gradient = product(0, j, inner)
        span = pl.ds(pl.multiple_of(j * CHUNK, CHUNK), CHUNK)
        grad[span] = gradient
        y_own[span] = jnp.zeros_like(gradient)
        for i in range(CHUNK // BLK):
            at = pl.ds(pl.multiple_of(j * CHUNK + i * BLK, BLK), BLK)
            step = mask_at(j * (CHUNK // BLK) + i) * gradient[i * BLK:(i + 1) * BLK]
            xo[1, row, at] = step.astype(jnp.bfloat16)
        send_own(1, j)

    send_inner(1)
    gather_and_multiply(1)
    inner = get_inner(1)

    def sums(j, carry):
        square, curve, curve_square = carry
        curvature = product(1, j, inner)
        span = pl.ds(pl.multiple_of(j * CHUNK, CHUNK), CHUNK)
        y_own[span] = curvature
        for i in range(CHUNK // BLK):
            at = pl.ds(pl.multiple_of(j * CHUNK + i * BLK, BLK), BLK)
            keep = mask_at(j * (CHUNK // BLK) + i)
            step = keep * grad[at]
            curved = curvature[i * BLK:(i + 1) * BLK]
            square = square + fold(step * step)
            curve = curve + fold(step * curved)
            curve_square = curve_square + fold((keep * curved) * (keep * curved))
        return square, curve, curve_square

    zero = jnp.zeros((8, width), jnp.float32)
    parts = lax.fori_loop(0, chunks, sums, (zero, zero, zero))
    tot_send[...] = jnp.concatenate(
        [jnp.sum(part, axis=0, keepdims=True) for part in parts] + [trace_row[0:1], zero[:4]], axis=0
    )
    tot_recv[me] = tot_send[...]
    for k in range(1, 2 * n):
        tot_copy(lax.rem(me + k, 2 * n), me).start()
    for k in range(1, 2 * n):
        peer = lax.rem(me + k, 2 * n)
        tot_copy(peer, peer).wait_recv()
    totals = jnp.sum(jnp.sum(tot_recv[...], axis=0), axis=1, keepdims=True)
    grad_square, grad_curve, curve_square, trace_total = (totals[i:i + 1] for i in range(4))
    damping = damping_ratio * trace_total / (n * rows)
    step_first = grad_square / (grad_curve + damping * grad_square + epsilon)
    step_second = (grad_curve + damping * grad_square) / (
        curve_square + 2.0 * damping * grad_curve + damping * damping * grad_square + epsilon
    )

    @pl.loop(0, blocks)
    def _(i):
        at = pl.ds(pl.multiple_of(i * BLK, BLK), BLK)
        keep = mask_at(i)
        gradient = grad[at]
        second = gradient - step_first * y_own[at]
        out[at] = keep * weights[at] - step_first * (keep * gradient) - step_second * (keep * second)

    for phase in range(2):
        @pl.loop(0, chunks)
        def _(j):
            for hop in range(last):
                for way in range(2):
                    ring(phase, way, hop, j).wait_send()

            @pl.when(j < split)
            def _():
                ring(phase, 0, last, j).wait_send()

            @pl.when(j >= split)
            def _():
                ring(phase, 1, last, j).wait_send()

            for b in range(nb):
                to_partner(phase, (1 - col) * nb + b, j).wait_send()
            y_copy(phase, j).wait_send()

        for k in range(1, n):
            peer = lax.rem(row + k, n)
            rs_copy(phase, peer, row).wait_send()
            ag_copy(phase, peer, row).wait_send()
    for k in range(1, 2 * n):
        tot_copy(lax.rem(me + k, 2 * n), me).wait_send()


def fused_device(gram_old, activations, weights, block_mask):
    n = lax.axis_size("row")
    rows, width = weights.shape
    depth = activations.shape[0]
    nb = gram_old.shape[1] // rows
    chunks = rows // CHUNK
    hops = n // 2
    piece = depth // n
    low, wide = jnp.bfloat16, jnp.float32
    dma = pltpu.SemaphoreType.DMA
    return pl.pallas_call(
        functools.partial(fused_kernel, n),
        out_shape=jax.ShapeDtypeStruct((rows, width), wide),
        in_specs=[
            pl.BlockSpec(memory_space=pl.ANY),
            pl.BlockSpec(memory_space=pltpu.VMEM),
            pl.BlockSpec(memory_space=pltpu.VMEM),
            pl.BlockSpec(memory_space=pltpu.SMEM),
        ],
        out_specs=pl.BlockSpec(memory_space=pltpu.VMEM),
        scratch_shapes=[
            pltpu.VMEM((nb, rows, rows), low),
            pltpu.VMEM((2, n, rows, width), low),
            pltpu.VMEM((2, nb, rows, width), low),
            pltpu.VMEM((rows, width), wide),
            pltpu.VMEM((2, rows, width), wide),
            pltpu.VMEM((2, rows, width), wide),
            pltpu.VMEM((rows, width), wide),
            pltpu.VMEM((2, n, piece, width), wide),
            pltpu.VMEM((2, n, piece, width), wide),
            pltpu.VMEM((2, piece, width), wide),
            pltpu.VMEM((2, n, piece, width), wide),
            pltpu.VMEM((8, width), wide),
            pltpu.VMEM((8, width), wide),
            pltpu.VMEM((2 * n, 8, width), wide),
            dma((nb,)),
            dma((2, 2, hops, chunks)),
            dma((2, 2, hops, chunks)),
            dma((2, nb, chunks)),
            dma((2, nb, chunks)),
            dma((2, chunks)),
            dma((2, chunks)),
            dma((2, n)),
            dma((2, n)),
            dma((2, n)),
            dma((2, n)),
            dma((2 * n,)),
            dma((2 * n,)),
        ],
        compiler_params=pltpu.CompilerParams(
            collective_id=0, has_side_effects=True, vmem_limit_bytes=62 * 1024 * 1024
        ),
        name="fused_steps",
    )(gram_old, activations, weights, block_mask)


def fits(gram_old, activations, weights, n):
    rows, width = weights.shape
    return (
        rows % CHUNK == 0
        and width == BLK
        and n % 4 == 0
        and gram_old.shape[1] == rows * n // 2
        and activations.shape[0] % (8 * n) == 0
        and gram_old.size <= 14 * 1024 * 1024
    )


def one_device(gram_old, activations, weights, block_mask):
    if fits(gram_old, activations, weights, lax.axis_size("row")):
        return fused_device(gram_old, activations, weights, block_mask)
    return per_device(gram_old, activations, weights, block_mask)


def solution(mesh):
    placed = (
        P(("groups", "row"), "col"),
        P("groups", "row"),
        P("row", ("groups", "col")),
        P(None, "groups"),
    )
    return jax.shard_map(
        one_device,
        mesh=mesh,
        in_specs=placed,
        out_specs=P("row", ("groups", "col")),
        check_vma=False,
    )
```

```python
import functools

import jax
import jax.numpy as jnp
from jax import lax
from jax.experimental import pallas as pl
from jax.experimental.pallas import tpu as pltpu
from jax.sharding import PartitionSpec as P

BLK = 128
CUTS = 2
MESH = pl.DeviceIdType.MESH
TRANSPOSED = (((0,), (0,)), ((), ()))


damping_ratio = 0.3
epsilon = 1e-06


def partner(value, axis, distance):
    return lax.ppermute(value, axis, [(i, i ^ 1 << distance) for i in range(lax.axis_size(axis))])


def expand_local(block_mask, row_offset, row_count, col_offset, col_count):
    row_ids = (row_offset + jnp.arange(row_count, dtype=jnp.int32)) // BLK
    col_ids = (col_offset + jnp.arange(col_count, dtype=jnp.int32)) // BLK
    pick_rows = (
        row_ids[:, None] == jnp.arange(block_mask.shape[0], dtype=jnp.int32)[None, :]
    ).astype(jnp.float32)
    pick_cols = (
        col_ids[:, None] == jnp.arange(block_mask.shape[1], dtype=jnp.int32)[None, :]
    ).astype(jnp.float32)
    partial_rows = jnp.dot(
        pick_rows, block_mask.astype(jnp.float32), precision=lax.Precision.HIGHEST
    )
    return jnp.dot(partial_rows, pick_cols.T, precision=lax.Precision.HIGHEST)


def update_product(activations, inner):
    high = inner.astype(jnp.bfloat16)
    low = (inner - high.astype(jnp.float32)).astype(jnp.bfloat16)
    contract = (((0,), (0,)), ((), ()))
    return lax.dot_general(
        activations, high, contract, preferred_element_type=jnp.float32
    ) + lax.dot_general(activations, low, contract, preferred_element_type=jnp.float32)


def per_device(gram_old, activations, weights, block_mask):
    row_block = gram_old.shape[0]
    half_width = gram_old.shape[1]
    width_cols = weights.shape[1]
    row_index = lax.axis_index("row")
    col_index = lax.axis_index("col")
    row_offset = row_index * row_block
    half_offset = col_index * half_width
    diag_column = row_offset + jnp.arange(row_block, dtype=jnp.int32) - half_offset
    on_diagonal = jnp.arange(half_width, dtype=jnp.int32)[None, :] == diag_column[:, None]
    trace_part = jnp.sum(jnp.where(on_diagonal, gram_old.astype(jnp.float32), 0.0))
    acts_wide = activations.astype(jnp.float32)
    trace_part = trace_part + jnp.sum(acts_wide * acts_wide) / lax.axis_size("col")
    mask_local = expand_local(block_mask, row_offset, row_block, col_index * width_cols, width_cols)

    def apply_gram(panel):
        panel_low = panel.astype(jnp.bfloat16)
        inner = lax.psum(
            jnp.dot(activations, panel_low, preferred_element_type=jnp.float32), "row"
        )
        low_rank = update_product(activations, inner)
        column_panel = lax.all_gather(panel_low, "row", axis=0, tiled=True)
        own_half = lax.dynamic_slice_in_dim(column_panel, half_offset, half_width, 0)
        partner_need = lax.dynamic_slice_in_dim(
            column_panel, (1 - col_index) * half_width, half_width, 0
        )
        partner_half = partner(partner_need, "col", 0)
        own_part = jnp.dot(gram_old, own_half, preferred_element_type=jnp.float32)
        partner_part = jnp.dot(gram_old, partner_half, preferred_element_type=jnp.float32)
        return own_part + partner(partner_part, "col", 0) + low_rank

    kept_weights = mask_local * weights
    pruned_diff = kept_weights - weights
    grad_first = apply_gram(pruned_diff)
    step_dir = mask_local * grad_first
    curvature = apply_gram(step_dir)
    masked_curve = mask_local * curvature
    local_square = jnp.sum(step_dir * step_dir)
    local_curve = jnp.sum(step_dir * curvature)
    local_curve_square = jnp.sum(masked_curve * masked_curve)
    grad_square, grad_curve, curve_square, trace_total = lax.psum(
        jnp.stack([local_square, local_curve, local_curve_square, trace_part]), ("row", "col")
    )
    damping = damping_ratio * trace_total / (row_block * lax.axis_size("row"))
    step_first = grad_square / (grad_curve + damping * grad_square + epsilon)
    step_second = (grad_curve + damping * grad_square) / (
        curve_square + 2.0 * damping * grad_curve + damping * damping * grad_square + epsilon
    )
    grad_second = grad_first - step_first * curvature
    return kept_weights - step_first * step_dir - step_second * (mask_local * grad_second)


def fused_kernel(
    n, gram, acts, weights, mask, out,
    g_vm, xo, xp, y_own, y_oth, y_rx, grad, red_send, red_recv,
    trace_row, tot_send, tot_recv,
    g_sem, ring_ssem, ring_rsem, par_ssem, par_rsem, y_ssem, y_rsem,
    red_ssem, red_rsem, tot_ssem, tot_rsem,
):
    rows, width = weights.shape
    nb = gram.shape[1] // rows
    nz = n // 2
    chunks = CUTS
    CHUNK = rows // CUTS
    split = (chunks + 1) // 2
    last = n // 2 - 1
    steps = red_send.shape[1]
    blocks = rows // BLK
    group = lax.axis_index("groups")
    row = lax.axis_index("row")
    col = lax.axis_index("col")
    near_half = row // nb

    def row_of(place):
        place = lax.rem(place + 2 * n, n)
        x = place // nz
        z = place + x * (n - 1 - 2 * place)
        return 2 * z + x

    my_z, my_x = row // 2, lax.rem(row, 2)
    place = my_z + my_x * (n - 1 - 2 * my_z)
    right, left = row_of(place + 1), row_of(place - 1)

    def mask_at(block):
        return mask[col, row * blocks + block].astype(jnp.float32)

    def ring(phase, way, hop, j):
        source = row_of(place - hop) if way == 0 else row_of(place + hop)
        part = xo.at[phase, source, pl.ds(pl.multiple_of(j * CHUNK, CHUNK), CHUNK)]
        return pltpu.make_async_remote_copy(
            src_ref=part, dst_ref=part,
            send_sem=ring_ssem.at[phase, way, hop, j], recv_sem=ring_rsem.at[phase, way, hop, j],
            device_id=(group, right if way == 0 else left, col), device_id_type=MESH,
        )

    def ring_arrival(phase, way, hop, j):
        source = row_of(place - hop - 1) if way == 0 else row_of(place + hop + 1)
        part = xo.at[phase, source, pl.ds(pl.multiple_of(j * CHUNK, CHUNK), CHUNK)]
        return pltpu.make_async_remote_copy(
            src_ref=part, dst_ref=part,
            send_sem=ring_ssem.at[phase, way, hop, j], recv_sem=ring_rsem.at[phase, way, hop, j],
            device_id=(group, right if way == 0 else left, col), device_id_type=MESH,
        )

    def to_partner(phase, source, j):
        span = pl.ds(pl.multiple_of(j * CHUNK, CHUNK), CHUNK)
        return pltpu.make_async_remote_copy(
            src_ref=xo.at[phase, source, span], dst_ref=xp.at[phase, lax.rem(source, nb), span],
            send_sem=par_ssem.at[phase, lax.rem(source, nb), j],
            recv_sem=par_rsem.at[phase, lax.rem(source, nb), j],
            device_id=(group, row, 1 - col), device_id_type=MESH,
        )

    def y_copy(phase, j):
        span = pl.ds(pl.multiple_of(j * CHUNK, CHUNK), CHUNK)
        return pltpu.make_async_remote_copy(
            src_ref=y_oth.at[phase, span], dst_ref=y_rx.at[phase, span],
            send_sem=y_ssem.at[phase, j], recv_sem=y_rsem.at[phase, j],
            device_id=(group, row, 1 - col), device_id_type=MESH,
        )

    def across(index, step):
        return index + (1 - 2 * lax.rem(index // 2 ** step, 2)) * 2 ** step

    def red_copy(phase, step):
        return pltpu.make_async_remote_copy(
            src_ref=red_send.at[phase, step], dst_ref=red_recv.at[phase, step],
            send_sem=red_ssem.at[phase, step], recv_sem=red_rsem.at[phase, step],
            device_id=(group, across(row, step), col), device_id_type=MESH,
        )

    me = row * 2 + col

    def tot_copy(step):
        peer = across(me, step)
        return pltpu.make_async_remote_copy(
            src_ref=tot_send.at[step], dst_ref=tot_recv.at[step],
            send_sem=tot_ssem.at[step], recv_sem=tot_rsem.at[step],
            device_id=(group, peer // 2, lax.rem(peer, 2)), device_id_type=MESH,
        )

    def gram_copy(b):
        return pltpu.make_async_copy(
            gram.at[:, pl.ds(pl.multiple_of(b * rows, rows), rows)], g_vm.at[b], g_sem.at[b]
        )

    def send_own(phase, j):
        @pl.when(near_half != col)
        def _():
            to_partner(phase, row, j).start()

        ring(phase, 0, 0, j).start()
        ring(phase, 1, 0, j).start()

    def send_inner(phase):
        red_send[phase, 0] = jnp.dot(
            acts[...], xo[phase, row], preferred_element_type=jnp.float32
        )
        red_copy(phase, 0).start()

    def reduce_inner(phase, step):
        red_copy(phase, step).wait_recv()
        return red_send[phase, step] + red_recv[phase, step]

    def add_update(phase):
        inner = reduce_inner(phase, steps - 1)
        high = inner.astype(jnp.bfloat16)
        low = (inner - high.astype(jnp.float32)).astype(jnp.bfloat16)
        pair = jnp.concatenate([high, low], axis=1)

        @pl.loop(0, blocks)
        def _(i):
            at = pl.ds(pl.multiple_of(i * BLK, BLK), BLK)
            both = lax.dot_general(
                acts[:, at], pair, TRANSPOSED, preferred_element_type=jnp.float32
            )
            y_own[at] += both[:, :width] + both[:, width:]

    def process(phase, source):
        @pl.when(source // nb == col)
        def _():
            for j in range(chunks):
                to_partner(phase, source, j).wait_recv()
            block = lax.rem(source, nb)
            panel = jnp.concatenate([xo[phase, source], xp[phase, block]], axis=1)

            @pl.loop(0, chunks)
            def _(tile):
                at = pl.ds(pl.multiple_of(tile * CHUNK, CHUNK), CHUNK)
                got = jnp.dot(g_vm[block, at], panel, preferred_element_type=jnp.float32)
                y_own[at] += got[:, :width]
                y_oth[phase, at] += got[:, width:]

    def relay(phase, source, j):
        @pl.when(source // nb != col)
        def _():
            to_partner(phase, source, j).start()

    def gather_and_multiply(phase):
        if phase == 0:
            gram_copy(lax.rem(row, nb)).wait()
        process(phase, row)
        if phase == 0:
            for b in range(1, nb):
                gram_copy(lax.rem(row + b, nb)).wait()
        for hop in range(last):
            for j in range(chunks):
                for way in range(2):
                    ring_arrival(phase, way, hop, j).wait_recv()
                    if hop + 1 < last or (j < split) == (way == 0):
                        ring(phase, way, hop + 1, j).start()
                    relay(phase, row_of(place + (2 * way - 1) * (hop + 1)), j)
            if hop < steps - 1:
                red_send[phase, hop + 1] = reduce_inner(phase, hop)
                red_copy(phase, hop + 1).start()

            @pl.loop(0, 2)
            def _(way):
                process(phase, row_of(place + (2 * way - 1) * (hop + 1)))
        add_update(phase)

        far = row_of(place + n // 2)
        for j in range(chunks):
            ring_arrival(phase, 0 if j < split else 1, last, j).wait_recv()
            relay(phase, far, j)
        block = lax.rem(far, nb)

        @pl.when(far // nb == col)
        def _():
            for j in range(chunks):
                to_partner(phase, far, j).wait_recv()
            panel = jnp.concatenate([xo[phase, far], xp[phase, block]], axis=1)

            @pl.loop(0, chunks)
            def _(j):
                at = pl.ds(pl.multiple_of(j * CHUNK, CHUNK), CHUNK)
                got = jnp.dot(g_vm[block, at], panel, preferred_element_type=jnp.float32)
                y_own[at] += got[:, :width]
                y_oth[phase, at] += got[:, width:]
                y_copy(phase, j).start()

        @pl.when(far // nb != col)
        def _():
            for j in range(chunks):
                y_copy(phase, j).start()

    def fold(values):
        return jnp.sum(values.reshape(-1, 8, width), axis=0)

    for b in range(nb):
        gram_copy(lax.rem(row + b, nb)).start()
    barrier = pltpu.get_barrier_semaphore()
    friends = [(right, col), (left, col), (row, 1 - col)]
    friends += [(across(row, step), col) for step in range(steps)]
    for friend in friends:
        pl.semaphore_signal(barrier, inc=1, device_id=(group, *friend), device_id_type=MESH)
    for i in range(blocks):
        at = pl.ds(i * BLK, BLK)
        w = weights[at]
        xo[0, row, at] = (mask_at(i) * w - w).astype(jnp.bfloat16)
    y_own[...] = jnp.zeros_like(y_own)
    y_oth[...] = jnp.zeros_like(y_oth)
    pl.semaphore_wait(barrier, len(friends))
    send_inner(0)
    for j in range(chunks):
        send_own(0, j)
    gather_and_multiply(0)

    per_chunk = CHUNK // BLK
    for j in range(chunks):
        y_copy(0, j).wait_recv()

        @pl.loop(j * per_chunk, (j + 1) * per_chunk)
        def _(i):
            at = pl.ds(pl.multiple_of(i * BLK, BLK), BLK)
            gradient = y_own[at] + y_rx[0, at]
            grad[at] = gradient
            y_own[at] = jnp.zeros_like(gradient)
            xo[1, row, at] = (mask_at(i) * gradient).astype(jnp.bfloat16)

        send_own(1, j)
    send_inner(1)
    trace_row[...] = jnp.zeros_like(trace_row)

    @pl.when(near_half == col)
    def _():
        own = lax.rem(row, nb)
        eye = lax.broadcasted_iota(jnp.int32, (BLK, BLK), 0) == lax.broadcasted_iota(
            jnp.int32, (BLK, BLK), 1
        )
        total = jnp.zeros((1, BLK), jnp.float32)
        for i in range(blocks):
            at = pl.ds(i * BLK, BLK)
            diagonal = jnp.where(eye, g_vm[own, at, at].astype(jnp.float32), 0.0)
            act = acts[:, at].astype(jnp.float32)
            total = total + jnp.sum(diagonal, axis=0, keepdims=True) + jnp.sum(
                act * act, axis=0, keepdims=True
            )
        trace_row[0:1] = total

    gather_and_multiply(1)

    def sums(i, carry):
        square, curve, curve_square = carry
        at = pl.ds(pl.multiple_of(i * BLK, BLK), BLK)
        curvature = y_own[at] + y_rx[1, at]
        y_own[at] = curvature
        keep = mask_at(i)
        step = keep * grad[at]
        square = square + fold(step * step)
        curve = curve + fold(step * curvature)
        curve_square = curve_square + fold((keep * curvature) * (keep * curvature))
        return square, curve, curve_square

    zero = jnp.zeros((8, width), jnp.float32)
    parts = (zero, zero, zero)
    for j in range(chunks):
        y_copy(1, j).wait_recv()
        parts = lax.fori_loop(j * per_chunk, (j + 1) * per_chunk, sums, parts)
    total = jnp.concatenate(
        [jnp.sum(part, axis=0, keepdims=True) for part in parts] + [trace_row[0:1], zero[:4]], axis=0
    )
    for step in range(steps + 1):
        tot_send[step] = total
        tot_copy(step).start()
        tot_copy(step).wait_recv()
        total = total + tot_recv[step]
    totals = jnp.sum(total, axis=1, keepdims=True)
    grad_square, grad_curve, curve_square, trace_total = (totals[i:i + 1] for i in range(4))
    damping = damping_ratio * trace_total / (n * rows)
    step_first = grad_square / (grad_curve + damping * grad_square + epsilon)
    step_second = (grad_curve + damping * grad_square) / (
        curve_square + 2.0 * damping * grad_curve + damping * damping * grad_square + epsilon
    )

    @pl.loop(0, blocks)
    def _(i):
        at = pl.ds(pl.multiple_of(i * BLK, BLK), BLK)
        keep = mask_at(i)
        gradient = grad[at]
        second = gradient - step_first * y_own[at]
        out[at] = keep * weights[at] - step_first * (keep * gradient) - step_second * (keep * second)

    for phase in range(2):
        for j in range(chunks):
            for hop in range(last):
                for way in range(2):
                    ring(phase, way, hop, j).wait_send()
            ring(phase, 0 if j < split else 1, last, j).wait_send()
            for b in range(nb):
                to_partner(phase, (1 - col) * nb + b, j).wait_send()
            y_copy(phase, j).wait_send()
        for step in range(steps):
            red_copy(phase, step).wait_send()
    for step in range(steps + 1):
        tot_copy(step).wait_send()


def fused_device(gram_old, activations, weights, block_mask):
    n = lax.axis_size("row")
    rows, width = weights.shape
    depth = activations.shape[0]
    nb = gram_old.shape[1] // rows
    chunks = CUTS
    hops = n // 2
    steps = n.bit_length() - 1
    low, wide = jnp.bfloat16, jnp.float32
    dma = pltpu.SemaphoreType.DMA
    return pl.pallas_call(
        functools.partial(fused_kernel, n),
        out_shape=jax.ShapeDtypeStruct((rows, width), wide),
        in_specs=[
            pl.BlockSpec(memory_space=pl.ANY),
            pl.BlockSpec(memory_space=pltpu.VMEM),
            pl.BlockSpec(memory_space=pltpu.VMEM),
            pl.BlockSpec(memory_space=pltpu.SMEM),
        ],
        out_specs=pl.BlockSpec(memory_space=pltpu.VMEM),
        scratch_shapes=[
            pltpu.VMEM((nb, rows, rows), low),
            pltpu.VMEM((2, n, rows, width), low),
            pltpu.VMEM((2, nb, rows, width), low),
            pltpu.VMEM((rows, width), wide),
            pltpu.VMEM((2, rows, width), wide),
            pltpu.VMEM((2, rows, width), wide),
            pltpu.VMEM((rows, width), wide),
            pltpu.VMEM((2, steps, depth, width), wide),
            pltpu.VMEM((2, steps, depth, width), wide),
            pltpu.VMEM((8, width), wide),
            pltpu.VMEM((steps + 1, 8, width), wide),
            pltpu.VMEM((steps + 1, 8, width), wide),
            dma((nb,)),
            dma((2, 2, hops, chunks)),
            dma((2, 2, hops, chunks)),
            dma((2, nb, chunks)),
            dma((2, nb, chunks)),
            dma((2, chunks)),
            dma((2, chunks)),
            dma((2, steps)),
            dma((2, steps)),
            dma((steps + 1,)),
            dma((steps + 1,)),
        ],
        compiler_params=pltpu.CompilerParams(
            collective_id=0, has_side_effects=True, vmem_limit_bytes=62 * 1024 * 1024
        ),
        name="fused_steps",
    )(gram_old, activations, weights, block_mask.T)


def fits(gram_old, activations, weights, n):
    rows, width = weights.shape
    return (
        rows % (CUTS * BLK) == 0
        and width == BLK
        and n >= 4
        and n & (n - 1) == 0
        and gram_old.shape[1] == rows * n // 2
        and activations.shape[0] % BLK == 0
        and gram_old.size <= 14 * 1024 * 1024
    )


def one_device(gram_old, activations, weights, block_mask):
    if fits(gram_old, activations, weights, lax.axis_size("row")):
        return fused_device(gram_old, activations, weights, block_mask)
    return per_device(gram_old, activations, weights, block_mask)


def solution(mesh):
    placed = (
        P(("groups", "row"), "col"),
        P("groups", "row"),
        P("row", ("groups", "col")),
        P(None, "groups"),
    )
    return jax.shard_map(
        one_device,
        mesh=mesh,
        in_specs=placed,
        out_specs=P("row", ("groups", "col")),
        check_vma=False,
    )
```

```python
import functools

import jax
import jax.numpy as jnp
from jax import lax
from jax.experimental import pallas as pl
from jax.experimental.pallas import tpu as pltpu
from jax.sharding import PartitionSpec as P

BLK = 128
CUTS = 2
MESH = pl.DeviceIdType.MESH
TRANSPOSED = (((0,), (0,)), ((), ()))


damping_ratio = 0.3
epsilon = 1e-06


def partner(value, axis, distance):
    return lax.ppermute(value, axis, [(i, i ^ 1 << distance) for i in range(lax.axis_size(axis))])


def expand_local(block_mask, row_offset, row_count, col_offset, col_count):
    row_ids = (row_offset + jnp.arange(row_count, dtype=jnp.int32)) // BLK
    col_ids = (col_offset + jnp.arange(col_count, dtype=jnp.int32)) // BLK
    pick_rows = (
        row_ids[:, None] == jnp.arange(block_mask.shape[0], dtype=jnp.int32)[None, :]
    ).astype(jnp.float32)
    pick_cols = (
        col_ids[:, None] == jnp.arange(block_mask.shape[1], dtype=jnp.int32)[None, :]
    ).astype(jnp.float32)
    partial_rows = jnp.dot(
        pick_rows, block_mask.astype(jnp.float32), precision=lax.Precision.HIGHEST
    )
    return jnp.dot(partial_rows, pick_cols.T, precision=lax.Precision.HIGHEST)


def update_product(activations, inner):
    high = inner.astype(jnp.bfloat16)
    low = (inner - high.astype(jnp.float32)).astype(jnp.bfloat16)
    contract = (((0,), (0,)), ((), ()))
    return lax.dot_general(
        activations, high, contract, preferred_element_type=jnp.float32
    ) + lax.dot_general(activations, low, contract, preferred_element_type=jnp.float32)


def per_device(gram_old, activations, weights, block_mask):
    row_block = gram_old.shape[0]
    half_width = gram_old.shape[1]
    width_cols = weights.shape[1]
    row_index = lax.axis_index("row")
    col_index = lax.axis_index("col")
    row_offset = row_index * row_block
    half_offset = col_index * half_width
    diag_column = row_offset + jnp.arange(row_block, dtype=jnp.int32) - half_offset
    on_diagonal = jnp.arange(half_width, dtype=jnp.int32)[None, :] == diag_column[:, None]
    trace_part = jnp.sum(jnp.where(on_diagonal, gram_old.astype(jnp.float32), 0.0))
    acts_wide = activations.astype(jnp.float32)
    trace_part = trace_part + jnp.sum(acts_wide * acts_wide) / lax.axis_size("col")
    mask_local = expand_local(block_mask, row_offset, row_block, col_index * width_cols, width_cols)

    def apply_gram(panel):
        panel_low = panel.astype(jnp.bfloat16)
        inner = lax.psum(
            jnp.dot(activations, panel_low, preferred_element_type=jnp.float32), "row"
        )
        low_rank = update_product(activations, inner)
        column_panel = lax.all_gather(panel_low, "row", axis=0, tiled=True)
        own_half = lax.dynamic_slice_in_dim(column_panel, half_offset, half_width, 0)
        partner_need = lax.dynamic_slice_in_dim(
            column_panel, (1 - col_index) * half_width, half_width, 0
        )
        partner_half = partner(partner_need, "col", 0)
        own_part = jnp.dot(gram_old, own_half, preferred_element_type=jnp.float32)
        partner_part = jnp.dot(gram_old, partner_half, preferred_element_type=jnp.float32)
        return own_part + partner(partner_part, "col", 0) + low_rank

    kept_weights = mask_local * weights
    pruned_diff = kept_weights - weights
    grad_first = apply_gram(pruned_diff)
    step_dir = mask_local * grad_first
    curvature = apply_gram(step_dir)
    masked_curve = mask_local * curvature
    local_square = jnp.sum(step_dir * step_dir)
    local_curve = jnp.sum(step_dir * curvature)
    local_curve_square = jnp.sum(masked_curve * masked_curve)
    grad_square, grad_curve, curve_square, trace_total = lax.psum(
        jnp.stack([local_square, local_curve, local_curve_square, trace_part]), ("row", "col")
    )
    damping = damping_ratio * trace_total / (row_block * lax.axis_size("row"))
    step_first = grad_square / (grad_curve + damping * grad_square + epsilon)
    step_second = (grad_curve + damping * grad_square) / (
        curve_square + 2.0 * damping * grad_curve + damping * damping * grad_square + epsilon
    )
    grad_second = grad_first - step_first * curvature
    return kept_weights - step_first * step_dir - step_second * (mask_local * grad_second)


def fused_kernel(
    n, gram, acts, weights, mask, out,
    g_vm, xo, xp, y_own, y_oth, y_rx, grad, red_send, red_recv,
    trace_row, tot_send, tot_recv,
    g_sem, ring_ssem, ring_rsem, par_ssem, par_rsem, y_ssem, y_rsem,
    red_ssem, red_rsem, tot_ssem, tot_rsem,
):
    rows, width = weights.shape
    nb = gram.shape[1] // rows
    nz = n // 2
    chunks = CUTS
    CHUNK = rows // CUTS
    split = (chunks + 1) // 2
    last = n // 2 - 1
    steps = red_send.shape[1]
    blocks = rows // BLK
    group = lax.axis_index("groups")
    row = lax.axis_index("row")
    col = lax.axis_index("col")
    near_half = row // nb

    def row_of(place):
        place = lax.rem(place + 2 * n, n)
        x = place // nz
        z = place + x * (n - 1 - 2 * place)
        return 2 * z + x

    my_z, my_x = row // 2, lax.rem(row, 2)
    place = my_z + my_x * (n - 1 - 2 * my_z)
    right, left = row_of(place + 1), row_of(place - 1)

    def mask_at(block):
        return mask[col, row * blocks + block].astype(jnp.float32)

    def ring(phase, way, hop, j):
        source = row_of(place - hop) if way == 0 else row_of(place + hop)
        part = xo.at[phase, source, pl.ds(pl.multiple_of(j * CHUNK, CHUNK), CHUNK)]
        return pltpu.make_async_remote_copy(
            src_ref=part, dst_ref=part,
            send_sem=ring_ssem.at[phase, way, hop, j], recv_sem=ring_rsem.at[phase, way, hop, j],
            device_id=(group, right if way == 0 else left, col), device_id_type=MESH,
        )

    def ring_arrival(phase, way, hop, j):
        source = row_of(place - hop - 1) if way == 0 else row_of(place + hop + 1)
        part = xo.at[phase, source, pl.ds(pl.multiple_of(j * CHUNK, CHUNK), CHUNK)]
        return pltpu.make_async_remote_copy(
            src_ref=part, dst_ref=part,
            send_sem=ring_ssem.at[phase, way, hop, j], recv_sem=ring_rsem.at[phase, way, hop, j],
            device_id=(group, right if way == 0 else left, col), device_id_type=MESH,
        )

    def to_partner(phase, source, j):
        span = pl.ds(pl.multiple_of(j * CHUNK, CHUNK), CHUNK)
        return pltpu.make_async_remote_copy(
            src_ref=xo.at[phase, source, span], dst_ref=xp.at[phase, lax.rem(source, nb), span],
            send_sem=par_ssem.at[phase, lax.rem(source, nb), j],
            recv_sem=par_rsem.at[phase, lax.rem(source, nb), j],
            device_id=(group, row, 1 - col), device_id_type=MESH,
        )

    def y_copy(phase, j):
        span = pl.ds(pl.multiple_of(j * CHUNK, CHUNK), CHUNK)
        return pltpu.make_async_remote_copy(
            src_ref=y_oth.at[phase, span], dst_ref=y_rx.at[phase, span],
            send_sem=y_ssem.at[phase, j], recv_sem=y_rsem.at[phase, j],
            device_id=(group, row, 1 - col), device_id_type=MESH,
        )

    def across(index, step):
        return index + (1 - 2 * lax.rem(index // 2 ** step, 2)) * 2 ** step

    def red_copy(phase, step):
        return pltpu.make_async_remote_copy(
            src_ref=red_send.at[phase, step], dst_ref=red_recv.at[phase, step],
            send_sem=red_ssem.at[phase, step], recv_sem=red_rsem.at[phase, step],
            device_id=(group, across(row, step), col), device_id_type=MESH,
        )

    me = row * 2 + col

    def tot_copy(step):
        peer = across(me, step)
        return pltpu.make_async_remote_copy(
            src_ref=tot_send.at[step], dst_ref=tot_recv.at[step],
            send_sem=tot_ssem.at[step], recv_sem=tot_rsem.at[step],
            device_id=(group, peer // 2, lax.rem(peer, 2)), device_id_type=MESH,
        )

    def gram_copy(b):
        return pltpu.make_async_copy(
            gram.at[:, pl.ds(pl.multiple_of(b * rows, rows), rows)], g_vm.at[b], g_sem.at[b]
        )

    def send_own(phase, j):
        @pl.when(near_half != col)
        def _():
            to_partner(phase, row, j).start()

        ring(phase, 0, 0, j).start()
        ring(phase, 1, 0, j).start()

    def send_inner(phase):
        red_send[phase, 0] = jnp.dot(
            acts[...], xo[phase, row], preferred_element_type=jnp.float32
        )
        red_copy(phase, 0).start()

    def reduce_inner(phase, step):
        red_copy(phase, step).wait_recv()
        return red_send[phase, step] + red_recv[phase, step]

    def add_update(phase):
        inner = reduce_inner(phase, steps - 1)
        high = inner.astype(jnp.bfloat16)
        low = (inner - high.astype(jnp.float32)).astype(jnp.bfloat16)
        pair = jnp.concatenate([high, low], axis=1)

        @pl.loop(0, blocks)
        def _(i):
            at = pl.ds(pl.multiple_of(i * BLK, BLK), BLK)
            both = lax.dot_general(
                acts[:, at], pair, TRANSPOSED, preferred_element_type=jnp.float32
            )
            y_own[at] += both[:, :width] + both[:, width:]

    def process(phase, source):
        @pl.when(source // nb == col)
        def _():
            for j in range(chunks):
                to_partner(phase, source, j).wait_recv()
            block = lax.rem(source, nb)
            panel = jnp.concatenate([xo[phase, source], xp[phase, block]], axis=1)

            @pl.loop(0, chunks)
            def _(tile):
                at = pl.ds(pl.multiple_of(tile * CHUNK, CHUNK), CHUNK)
                got = jnp.dot(g_vm[block, at], panel, preferred_element_type=jnp.float32)
                y_own[at] += got[:, :width]
                y_oth[phase, at] += got[:, width:]

    def relay(phase, source, j):
        @pl.when(source // nb != col)
        def _():
            to_partner(phase, source, j).start()

    def gather_and_multiply(phase):
        if phase == 0:
            gram_copy(lax.rem(row, nb)).wait()
        process(phase, row)
        if phase == 0:
            for b in range(1, nb):
                gram_copy(lax.rem(row + b, nb)).wait()
        for hop in range(last):
            for j in range(chunks):
                for way in range(2):
                    ring_arrival(phase, way, hop, j).wait_recv()
                    if hop + 1 < last or (j < split) == (way == 0):
                        ring(phase, way, hop + 1, j).start()
                    relay(phase, row_of(place + (2 * way - 1) * (hop + 1)), j)
            if hop < steps - 1:
                red_send[phase, hop + 1] = reduce_inner(phase, hop)
                red_copy(phase, hop + 1).start()

            @pl.loop(0, 2)
            def _(way):
                process(phase, row_of(place + (2 * way - 1) * (hop + 1)))
        add_update(phase)

        far = row_of(place + n // 2)
        for j in range(chunks):
            ring_arrival(phase, 0 if j < split else 1, last, j).wait_recv()
            relay(phase, far, j)
        block = lax.rem(far, nb)

        @pl.when(far // nb == col)
        def _():
            for j in range(chunks):
                to_partner(phase, far, j).wait_recv()
            panel = jnp.concatenate([xo[phase, far], xp[phase, block]], axis=1)

            @pl.loop(0, chunks)
            def _(j):
                at = pl.ds(pl.multiple_of(j * CHUNK, CHUNK), CHUNK)
                got = jnp.dot(g_vm[block, at], panel, preferred_element_type=jnp.float32)
                y_own[at] += got[:, :width]
                y_oth[phase, at] += got[:, width:]
                y_copy(phase, j).start()

        @pl.when(far // nb != col)
        def _():
            for j in range(chunks):
                y_copy(phase, j).start()

    def fold(values):
        return jnp.sum(values.reshape(-1, 8, width), axis=0)

    for b in range(nb):
        gram_copy(lax.rem(row + b, nb)).start()
    barrier = pltpu.get_barrier_semaphore()
    friends = [(right, col), (left, col), (row, 1 - col)]
    friends += [(across(row, step), col) for step in range(steps)]
    for friend in friends:
        pl.semaphore_signal(barrier, inc=1, device_id=(group, *friend), device_id_type=MESH)
    for i in range(blocks):
        at = pl.ds(i * BLK, BLK)
        w = weights[at]
        xo[0, row, at] = (mask_at(i) * w - w).astype(jnp.bfloat16)
    y_own[...] = jnp.zeros_like(y_own)
    y_oth[...] = jnp.zeros_like(y_oth)
    pl.semaphore_wait(barrier, len(friends))
    for j in range(chunks):
        send_own(0, j)
    send_inner(0)
    gather_and_multiply(0)

    per_chunk = CHUNK // BLK
    for j in range(chunks):
        y_copy(0, j).wait_recv()

        @pl.loop(j * per_chunk, (j + 1) * per_chunk)
        def _(i):
            at = pl.ds(pl.multiple_of(i * BLK, BLK), BLK)
            gradient = y_own[at] + y_rx[0, at]
            grad[at] = gradient
            y_own[at] = jnp.zeros_like(gradient)
            xo[1, row, at] = (mask_at(i) * gradient).astype(jnp.bfloat16)

        send_own(1, j)
    send_inner(1)
    trace_row[...] = jnp.zeros_like(trace_row)

    @pl.when(near_half == col)
    def _():
        own = lax.rem(row, nb)
        eye = lax.broadcasted_iota(jnp.int32, (BLK, BLK), 0) == lax.broadcasted_iota(
            jnp.int32, (BLK, BLK), 1
        )
        total = jnp.zeros((1, BLK), jnp.float32)
        for i in range(blocks):
            at = pl.ds(i * BLK, BLK)
            diagonal = jnp.where(eye, g_vm[own, at, at].astype(jnp.float32), 0.0)
            act = acts[:, at].astype(jnp.float32)
            total = total + jnp.sum(diagonal, axis=0, keepdims=True) + jnp.sum(
                act * act, axis=0, keepdims=True
            )
        trace_row[0:1] = total

    gather_and_multiply(1)

    def sums(i, carry):
        square, curve, curve_square = carry
        at = pl.ds(pl.multiple_of(i * BLK, BLK), BLK)
        curvature = y_own[at] + y_rx[1, at]
        y_own[at] = curvature
        keep = mask_at(i)
        step = keep * grad[at]
        square = square + fold(step * step)
        curve = curve + fold(step * curvature)
        curve_square = curve_square + fold((keep * curvature) * (keep * curvature))
        return square, curve, curve_square

    zero = jnp.zeros((8, width), jnp.float32)
    parts = (zero, zero, zero)
    for j in range(chunks):
        y_copy(1, j).wait_recv()
        parts = lax.fori_loop(j * per_chunk, (j + 1) * per_chunk, sums, parts)
    total = jnp.concatenate(
        [jnp.sum(part, axis=0, keepdims=True) for part in parts] + [trace_row[0:1], zero[:4]], axis=0
    )
    for step in range(steps + 1):
        tot_send[step] = total
        tot_copy(step).start()
        tot_copy(step).wait_recv()
        total = total + tot_recv[step]
    totals = jnp.sum(total, axis=1, keepdims=True)
    grad_square, grad_curve, curve_square, trace_total = (totals[i:i + 1] for i in range(4))
    damping = damping_ratio * trace_total / (n * rows)
    step_first = grad_square / (grad_curve + damping * grad_square + epsilon)
    step_second = (grad_curve + damping * grad_square) / (
        curve_square + 2.0 * damping * grad_curve + damping * damping * grad_square + epsilon
    )

    @pl.loop(0, blocks)
    def _(i):
        at = pl.ds(pl.multiple_of(i * BLK, BLK), BLK)
        keep = mask_at(i)
        gradient = grad[at]
        second = gradient - step_first * y_own[at]
        out[at] = keep * weights[at] - step_first * (keep * gradient) - step_second * (keep * second)

    for phase in range(2):
        for j in range(chunks):
            for hop in range(last):
                for way in range(2):
                    ring(phase, way, hop, j).wait_send()
            ring(phase, 0 if j < split else 1, last, j).wait_send()
            for b in range(nb):
                to_partner(phase, (1 - col) * nb + b, j).wait_send()
            y_copy(phase, j).wait_send()
        for step in range(steps):
            red_copy(phase, step).wait_send()
    for step in range(steps + 1):
        tot_copy(step).wait_send()


def fused_device(gram_old, activations, weights, block_mask):
    n = lax.axis_size("row")
    rows, width = weights.shape
    depth = activations.shape[0]
    nb = gram_old.shape[1] // rows
    chunks = CUTS
    hops = n // 2
    steps = n.bit_length() - 1
    low, wide = jnp.bfloat16, jnp.float32
    dma = pltpu.SemaphoreType.DMA
    return pl.pallas_call(
        functools.partial(fused_kernel, n),
        out_shape=jax.ShapeDtypeStruct((rows, width), wide),
        in_specs=[
            pl.BlockSpec(memory_space=pl.ANY),
            pl.BlockSpec(memory_space=pltpu.VMEM),
            pl.BlockSpec(memory_space=pltpu.VMEM),
            pl.BlockSpec(memory_space=pltpu.SMEM),
        ],
        out_specs=pl.BlockSpec(memory_space=pltpu.VMEM),
        scratch_shapes=[
            pltpu.VMEM((nb, rows, rows), low),
            pltpu.VMEM((2, n, rows, width), low),
            pltpu.VMEM((2, nb, rows, width), low),
            pltpu.VMEM((rows, width), wide),
            pltpu.VMEM((2, rows, width), wide),
            pltpu.VMEM((2, rows, width), wide),
            pltpu.VMEM((rows, width), wide),
            pltpu.VMEM((2, steps, depth, width), wide),
            pltpu.VMEM((2, steps, depth, width), wide),
            pltpu.VMEM((8, width), wide),
            pltpu.VMEM((steps + 1, 8, width), wide),
            pltpu.VMEM((steps + 1, 8, width), wide),
            dma((nb,)),
            dma((2, 2, hops, chunks)),
            dma((2, 2, hops, chunks)),
            dma((2, nb, chunks)),
            dma((2, nb, chunks)),
            dma((2, chunks)),
            dma((2, chunks)),
            dma((2, steps)),
            dma((2, steps)),
            dma((steps + 1,)),
            dma((steps + 1,)),
        ],
        compiler_params=pltpu.CompilerParams(
            collective_id=0, has_side_effects=True, vmem_limit_bytes=62 * 1024 * 1024
        ),
        name="fused_steps",
    )(gram_old, activations, weights, block_mask.T)


def fits(gram_old, activations, weights, n):
    rows, width = weights.shape
    return (
        rows % (CUTS * BLK) == 0
        and width == BLK
        and n >= 4
        and n & (n - 1) == 0
        and gram_old.shape[1] == rows * n // 2
        and activations.shape[0] % BLK == 0
        and gram_old.size <= 14 * 1024 * 1024
    )


def one_device(gram_old, activations, weights, block_mask):
    if fits(gram_old, activations, weights, lax.axis_size("row")):
        return fused_device(gram_old, activations, weights, block_mask)
    return per_device(gram_old, activations, weights, block_mask)


def solution(mesh):
    placed = (
        P(("groups", "row"), "col"),
        P("groups", "row"),
        P("row", ("groups", "col")),
        P(None, "groups"),
    )
    return jax.shard_map(
        one_device,
        mesh=mesh,
        in_specs=placed,
        out_specs=P("row", ("groups", "col")),
        check_vma=False,
    )
```
